32 devices in a mesh: sect: 2 (over x), slab: 8 (over z, y), energy: 2 (over core).
Axes of the slice: x: 2, y: 2, z: 4, core: 2. Of those that a mesh axis runs over, the one named last changes fastest.
Arguments:
- source: bfloat16 [4, 512, 128], P(('energy', 'sect'), 'slab'), parts along dimension 0, may hold values from -6 to 6
- forward_mult: bfloat16 [4, 2, 512, 512], P(('energy', 'sect'), None, 'slab'), parts along dimension 0, may hold values from -0.1875 to 0.1875
- schur_inverse: bfloat16 [4, 2, 512, 512], P(('energy', 'sect'), None, 'slab'), parts along dimension 0, may hold values from -0.09375 to 0.09375
- upper_mult: bfloat16 [4, 2, 512, 512], P(('energy', 'sect'), None, 'slab'), parts along dimension 0, may hold values from -0.125 to 0.125
Outputs:
- wave: bfloat16 [4, 512, 128], P(('energy', 'sect'), 'slab'), parts along dimension 0
The draws below stay inside these ranges and needn't reach their ends.
There are 2 independent parts, one for each index of `energy`. The reference program is written for one: setup_inputs(seed, part) draws one part's arguments, and reference() takes and returns one part's arrays. A program takes and returns all parts, laid end to end along the dimension named above; each array names one. Nothing has to cross between parts.
All inputs are finite; a program needn't handle non-finite values.
Results may differ from the reference program's by a relative error of at most 0.012.
Values may be sent and summed in bfloat16 or wider, within the bound.
No kernel may reach another device: no remote copies, remote signals or barrier semaphores. Data moves between devices by JAX's collectives and lax.ppermute only.
A program may use at most 64 MiB of HBM per device.

```python
import jax
import jax.numpy as jnp

MODES = 64
ORDER = 512
SECTIONS = 2


def shard_levels(key, dims, pieces, least, high):
    def one(position, shards_of):
        steps = jax.random.uniform(jax.random.fold_in(jax.random.fold_in(key, 6), position), (shards_of,), jnp.float32, least / len(pieces), high / len(pieces))
        return jnp.repeat(jnp.exp(steps), dims[position] // shards_of).reshape((-1,) + (1,) * (len(dims) - position - 1))

    factor_of = one(*pieces[0])
    for cut in pieces[1:]:
        factor_of = factor_of * one(*cut)
    return factor_of


def noise(stream_key, dims, scale, reach, pieces=(), held_as=jnp.bfloat16):
    drawn = scale * jax.random.normal(stream_key, dims, jnp.float32)
    if pieces:
        drawn = drawn * shard_levels(stream_key, dims, pieces, -0.22, 0.18)
    return jnp.clip(drawn, -reach, reach).astype(held_as)


def setup_inputs(seed: int = 0, part: int = 0) -> dict:
    key_of = jax.random.split(jax.random.key(seed), 5)
    own_keys = jax.random.split(jax.random.fold_in(key_of[4], part), 5)
    source = noise(own_keys[0], (SECTIONS, ORDER, 2 * MODES), 1.0, 6.0, ((0, 2), (1, 8)))
    forward_mult = noise(own_keys[1], (SECTIONS, 2, ORDER, ORDER), (2 * ORDER) ** -0.5, 0.1875, ((0, 2), (2, 8)))
    schur_inverse = noise(own_keys[2], (SECTIONS, 2, ORDER, ORDER), (8 * ORDER) ** -0.5, 0.09375, ((0, 2), (2, 8)))
    upper_mult = noise(own_keys[3], (SECTIONS, 2, ORDER, ORDER), (4 * ORDER) ** -0.5, 0.125, ((0, 2), (2, 8)))
    return {"source": source, "forward_mult": forward_mult, "schur_inverse": schur_inverse, "upper_mult": upper_mult}


def complex_apply(matrix, vector):
    half_cols = vector.shape[1] // 2
    real_part = jnp.dot(matrix[0], vector, preferred_element_type=jnp.float32)
    imag_part = jnp.dot(matrix[1], vector, preferred_element_type=jnp.float32)
    return jnp.concatenate([real_part[:, :half_cols] - imag_part[:, half_cols:], real_part[:, half_cols:] + imag_part[:, :half_cols]], axis=1)


def reference(source, forward_mult, schur_inverse, upper_mult):
    sections = source.shape[0]
    previous = jnp.zeros_like(source[0])
    forward_list = []
    for section in range(sections):
        previous = (source[section].astype(jnp.float32) + complex_apply(forward_mult[section], previous)).astype(jnp.bfloat16)
        forward_list.append(previous)
    following = jnp.zeros_like(source[0])
    waves = [following] * sections
    for section in reversed(range(sections)):
        scaled = complex_apply(schur_inverse[section], forward_list[section])
        following = (scaled - complex_apply(upper_mult[section], following)).astype(jnp.bfloat16)
        waves[section] = following
    return jnp.stack(waves)
```

```python
import jax
import jax.numpy as jnp
from jax import lax
from jax.sharding import PartitionSpec as P


def from_behind(block, axis, distance):
    devices = range(lax.axis_size(axis))
    route = [(i - distance, i) for i in devices if i - distance in devices]
    return lax.ppermute(block, axis, route)


def gather_rows(rows):
    devices = lax.axis_size("slab")
    copies = jnp.broadcast_to(rows[None], (devices,) + rows.shape)
    blocks = lax.all_to_all(copies, "slab", split_axis=0, concat_axis=0)
    return blocks.reshape((devices * rows.shape[0],) + rows.shape[1:])


def complex_apply(matrix, vector):
    rows, half_cols = matrix.shape[0] // 2, vector.shape[1] // 2
    both = jnp.dot(matrix, vector, preferred_element_type=jnp.float32)
    real_part, imag_part = both[:rows], both[rows:]
    return jnp.concatenate(
        [
            real_part[:, :half_cols] - imag_part[:, half_cols:],
            real_part[:, half_cols:] + imag_part[:, :half_cols],
        ],
        axis=1,
    )


def two_sections(src, forward, inverse, upper):
    first = lax.axis_index("sect") == 0
    height, order = forward.shape
    flat = src.reshape(-1, order)
    bundle = jnp.concatenate([forward, inverse, flat], axis=0)
    other = lax.ppermute(bundle, "sect", [(0, 1), (1, 0)])
    src_all = gather_rows(src)
    other_forward, other_inverse = other[:height], other[height : 2 * height]
    other_src = other[2 * height :].reshape(src.shape)

    next_forward = (other_src.astype(jnp.float32) + complex_apply(other_forward, src_all)).astype(jnp.bfloat16)
    scaled = complex_apply(inverse, src_all)

    second = gather_rows(jnp.where(first, next_forward, other_src))
    matrix = jnp.where(first, other_inverse, forward)
    added = jnp.where(first, jnp.zeros_like(src), src).astype(jnp.float32)
    rows = (added + complex_apply(matrix, second)).astype(jnp.bfloat16)

    third = gather_rows(rows)
    matrix = jnp.where(first, upper, inverse)
    product = complex_apply(matrix, third)
    return jnp.where(first, scaled - product, product).astype(jnp.bfloat16)


def many_sections(src, forward, inverse, upper):
    sections = lax.axis_size("sect")
    src_float = src.astype(jnp.float32)

    def forward_segment(segment_no, current):
        inflow = from_behind(current, "sect", 1)
        return (src_float + complex_apply(forward, gather_rows(inflow))).astype(jnp.bfloat16)

    forward_rows = lax.fori_loop(1, sections, forward_segment, src)
    scaled = complex_apply(inverse, gather_rows(forward_rows))

    def backward_segment(segment_no, current):
        outflow = from_behind(current, "sect", -1)
        return (scaled - complex_apply(upper, gather_rows(outflow))).astype(jnp.bfloat16)

    return lax.fori_loop(1, sections, backward_segment, scaled.astype(jnp.bfloat16))


def per_device(source, forward_mult, schur_inverse, upper_mult):
    src = source[0]
    forward, inverse, upper = (m[0].reshape(-1, m.shape[-1]) for m in (forward_mult, schur_inverse, upper_mult))
    fits = src.size % forward.shape[-1] == 0
    run = two_sections if lax.axis_size("sect") == 2 and fits else many_sections
    return run(src, forward, inverse, upper)[None]


def solution(mesh):
    in_specs = (
        P(("energy", "sect"), "slab", None),
        P(("energy", "sect"), None, "slab", None),
        P(("energy", "sect"), None, "slab", None),
        P(("energy", "sect"), None, "slab", None),
    )
    out_specs = P(("energy", "sect"), "slab", None)
    return jax.shard_map(
        per_device, mesh=mesh, in_specs=in_specs, out_specs=out_specs, check_vma=False
    )
```

```python
import jax
import jax.numpy as jnp
from jax import lax
from jax.sharding import PartitionSpec as P


def from_behind(block, axis, distance):
    devices = range(lax.axis_size(axis))
    route = [(i - distance, i) for i in devices if i - distance in devices]
    return lax.ppermute(block, axis, route)


def gather_rows(rows):
    devices = lax.axis_size("slab")
    middle = devices // 2 + 1 if devices > 2 else 0
    order = [(middle - i) % devices for i in range(devices)]
    copies = jnp.broadcast_to(rows[None], (devices,) + rows.shape)
    blocks = lax.all_to_all(copies, "slab", split_axis=0, concat_axis=0, axis_index_groups=[order])
    return [blocks[order.index(i)] for i in range(devices)]


def complex_apply(matrix, blocks):
    vector = jnp.concatenate(blocks, axis=0)
    rows, half_cols = matrix.shape[0] // 2, vector.shape[1] // 2
    both = jnp.dot(matrix, vector, preferred_element_type=jnp.float32)
    real_part, imag_part = both[:rows], both[rows:]
    return jnp.concatenate(
        [
            real_part[:, :half_cols] - imag_part[:, half_cols:],
            real_part[:, half_cols:] + imag_part[:, :half_cols],
        ],
        axis=1,
    )


def two_sections(src, forward, inverse, upper):
    swap = [(0, 1), (1, 0)]
    first = lax.axis_index("sect") == 0
    other_forward = lax.ppermute(forward, "sect", swap)
    other_src = lax.ppermute(src, "sect", swap)
    other_inverse = lax.ppermute(inverse, "sect", swap)
    src_blocks = gather_rows(src)
    last = jnp.where(
        first,
        jnp.concatenate([inverse, -upper], axis=1),
        jnp.concatenate([jnp.zeros_like(inverse), inverse], axis=1),
    )
    mine = jnp.where(first, jnp.zeros_like(forward), forward)
    added = jnp.where(first, jnp.zeros_like(src), src).astype(jnp.float32)
    other_forward, other_src, src_blocks, last, mine, added = lax.optimization_barrier(
        (other_forward, other_src, src_blocks, last, mine, added)
    )

    next_forward = (other_src.astype(jnp.float32) + complex_apply(other_forward, src_blocks)).astype(jnp.bfloat16)
    second = gather_rows(jnp.where(first, next_forward, other_src))

    other_inverse, second = lax.optimization_barrier((other_inverse, second))
    matrix = jnp.where(first, other_inverse, mine)
    rows = (added + complex_apply(matrix, second)).astype(jnp.bfloat16)

    third = gather_rows(rows)
    return complex_apply(last, src_blocks + third).astype(jnp.bfloat16)


def many_sections(src, forward, inverse, upper):
    sections = lax.axis_size("sect")
    src_float = src.astype(jnp.float32)

    def forward_segment(segment_no, current):
        inflow = from_behind(current, "sect", 1)
        return (src_float + complex_apply(forward, gather_rows(inflow))).astype(jnp.bfloat16)

    forward_rows = lax.fori_loop(1, sections, forward_segment, src)
    scaled = complex_apply(inverse, gather_rows(forward_rows))

    def backward_segment(segment_no, current):
        outflow = from_behind(current, "sect", -1)
        return (scaled - complex_apply(upper, gather_rows(outflow))).astype(jnp.bfloat16)

    return lax.fori_loop(1, sections, backward_segment, scaled.astype(jnp.bfloat16))


def per_device(source, forward_mult, schur_inverse, upper_mult):
    src = source[0]
    forward, inverse, upper = (m[0].reshape(-1, m.shape[-1]) for m in (forward_mult, schur_inverse, upper_mult))
    run = two_sections if lax.axis_size("sect") == 2 else many_sections
    return run(src, forward, inverse, upper)[None]


def solution(mesh):
    in_specs = (
        P(("energy", "sect"), "slab", None),
        P(("energy", "sect"), None, "slab", None),
        P(("energy", "sect"), None, "slab", None),
        P(("energy", "sect"), None, "slab", None),
    )
    out_specs = P(("energy", "sect"), "slab", None)
    return jax.shard_map(
        per_device, mesh=mesh, in_specs=in_specs, out_specs=out_specs, check_vma=False
    )
```

```python
import jax
import jax.numpy as jnp
from jax import lax
from jax.experimental import pallas as pl
from jax.experimental.pallas import tpu as pltpu
from jax.sharding import PartitionSpec as P


def from_behind(block, axis, distance):
    devices = range(lax.axis_size(axis))
    route = [(i - distance, i) for i in devices if i - distance in devices]
    return lax.ppermute(block, axis, route)


def group_order(devices):
    middle = devices // 2 + 1 if devices > 2 else 0
    return [(middle - i) % devices for i in range(devices)]


def exchange(copies):
    order = group_order(copies.shape[0])
    return lax.all_to_all(copies, "slab", split_axis=0, concat_axis=0, axis_index_groups=[order])


def gather_rows(rows):
    devices = lax.axis_size("slab")
    blocks = exchange(jnp.broadcast_to(rows[None], (devices,) + rows.shape))
    order = group_order(devices)
    return [blocks[order.index(i)] for i in range(devices)]


def complex_apply(matrix, blocks):
    vector = jnp.concatenate(blocks, axis=0)
    rows, half_cols = matrix.shape[0] // 2, vector.shape[1] // 2
    both = jnp.dot(matrix, vector, preferred_element_type=jnp.float32)
    real_part, imag_part = both[:rows], both[rows:]
    return jnp.concatenate(
        [
            real_part[:, :half_cols] - imag_part[:, half_cols:],
            real_part[:, half_cols:] + imag_part[:, :half_cols],
        ],
        axis=1,
    )


def in_order(blocks_ref):
    devices = blocks_ref.shape[0]
    order = group_order(devices)
    return [blocks_ref[order.index(i)] for i in range(devices)]


def hand_out(copies_ref, rows):
    for i in range(copies_ref.shape[0]):
        copies_ref[i] = rows


def prepare_kernel(src_ref, forward_ref, inverse_ref, upper_ref, bundle_ref, upper_out_ref, copies_ref, sems):
    height, order = forward_ref.shape
    rows = src_ref.shape[0]
    pairs = [
        (src_ref, bundle_ref.at[pl.ds(0, rows), pl.ds(2 * order, src_ref.shape[1])]),
        (src_ref, copies_ref.at[0]),
        (forward_ref, bundle_ref.at[:, pl.ds(0, order)]),
        (inverse_ref, bundle_ref.at[:, pl.ds(order, order)]),
        (upper_ref, upper_out_ref),
    ]
    copies = [pltpu.make_async_copy(a, b, sems.at[i]) for i, (a, b) in enumerate(pairs)]
    for copy in copies:
        copy.start()
    if height > rows:
        bundle_ref[rows:, 2 * order :] = jnp.zeros((height - rows, src_ref.shape[1]), bundle_ref.dtype)
    copies[0].wait()
    copies[1].wait()
    rows_in = copies_ref[0]
    for i in range(1, copies_ref.shape[0]):
        copies_ref[i] = rows_in
    for copy in copies[2:]:
        copy.wait()


def forward_kernel(other_ref, blocks_ref, copies_ref):
    order = blocks_ref.shape[0] * blocks_ref.shape[1]
    other_src = other_ref[: blocks_ref.shape[1], 2 * order :]
    first = lax.axis_index("sect") == 0

    @pl.when(first)
    def _():
        made = other_src.astype(jnp.float32) + complex_apply(other_ref[:, :order], in_order(blocks_ref))
        hand_out(copies_ref, made.astype(copies_ref.dtype))

    @pl.when(jnp.logical_not(first))
    def _():
        hand_out(copies_ref, other_src)


def wave_kernel(other_ref, bundle_ref, blocks_ref, copies_ref):
    order = blocks_ref.shape[0] * blocks_ref.shape[1]
    first = lax.axis_index("sect") == 0

    @pl.when(first)
    def _():
        made = complex_apply(other_ref[:, order : 2 * order], in_order(blocks_ref))
        hand_out(copies_ref, -made.astype(copies_ref.dtype))

    @pl.when(jnp.logical_not(first))
    def _():
        own_src = bundle_ref[: blocks_ref.shape[1], 2 * order :]
        made = own_src.astype(jnp.float32) + complex_apply(bundle_ref[:, :order], in_order(blocks_ref))
        hand_out(copies_ref, made.astype(copies_ref.dtype))


def last_kernel(bundle_ref, upper_ref, src_blocks_ref, blocks_ref, out_ref):
    order = blocks_ref.shape[0] * blocks_ref.shape[1]
    inverse = bundle_ref[:, order : 2 * order]
    first = lax.axis_index("sect") == 0

    @pl.when(first)
    def _():
        made = complex_apply(inverse, in_order(src_blocks_ref)) + complex_apply(upper_ref[...], in_order(blocks_ref))
        out_ref[...] = made.astype(out_ref.dtype)

    @pl.when(jnp.logical_not(first))
    def _():
        out_ref[...] = complex_apply(inverse, in_order(blocks_ref)).astype(out_ref.dtype)


def two_sections(src, forward, inverse, upper):
    devices = lax.axis_size("slab")
    height, order = forward.shape
    vmem = pl.BlockSpec(memory_space=pltpu.VMEM)
    small = pltpu.CompilerParams(vmem_limit_bytes=8 * 1024 * 1024)
    copies_shape = jax.ShapeDtypeStruct((devices,) + src.shape, src.dtype)
    bundle_shape = jax.ShapeDtypeStruct((height, 2 * order + src.shape[1]), src.dtype)
    bundle, upper, copies = pl.pallas_call(
        prepare_kernel,
        in_specs=[pl.BlockSpec(memory_space=pltpu.HBM)] * 4,
        out_specs=[vmem] * 3,
        out_shape=[bundle_shape, jax.ShapeDtypeStruct(upper.shape, upper.dtype), copies_shape],
        scratch_shapes=[pltpu.SemaphoreType.DMA((5,))],
        compiler_params=small, name="prepare",
    )(*(pltpu.with_memory_space_constraint(array, pltpu.HBM) for array in (src, forward, inverse, upper)))
    other = lax.ppermute(bundle, "sect", [(0, 1), (1, 0)])
    src_blocks = exchange(copies)
    other, src_blocks = lax.optimization_barrier((other, src_blocks))

    copies = pl.pallas_call(
        forward_kernel, in_specs=[vmem] * 2, out_specs=vmem, out_shape=copies_shape, compiler_params=small, name="forward"
    )(other, src_blocks)
    second = exchange(copies)
    copies = pl.pallas_call(
        wave_kernel, in_specs=[vmem] * 3, out_specs=vmem, out_shape=copies_shape, compiler_params=small, name="wave"
    )(other, bundle, second)
    third = exchange(copies)
    return pl.pallas_call(
        last_kernel, in_specs=[vmem] * 4, out_specs=vmem, out_shape=jax.ShapeDtypeStruct(src.shape, src.dtype), compiler_params=small, name="last"
    )(bundle, upper, src_blocks, third)


def many_sections(src, forward, inverse, upper):
    sections = lax.axis_size("sect")
    src_float = src.astype(jnp.float32)

    def forward_segment(segment_no, current):
        inflow = from_behind(current, "sect", 1)
        return (src_float + complex_apply(forward, gather_rows(inflow))).astype(jnp.bfloat16)

    forward_rows = lax.fori_loop(1, sections, forward_segment, src)
    scaled = complex_apply(inverse, gather_rows(forward_rows))

    def backward_segment(segment_no, current):
        outflow = from_behind(current, "sect", -1)
        return (scaled - complex_apply(upper, gather_rows(outflow))).astype(jnp.bfloat16)

    return lax.fori_loop(1, sections, backward_segment, scaled.astype(jnp.bfloat16))


def per_device(source, forward_mult, schur_inverse, upper_mult):
    src = source[0]
    forward, inverse, upper = (m[0].reshape(-1, m.shape[-1]) for m in (forward_mult, schur_inverse, upper_mult))
    run = two_sections if lax.axis_size("sect") == 2 else many_sections
    return run(src, forward, inverse, upper)[None]


def solution(mesh):
    in_specs = (
        P(("energy", "sect"), "slab", None),
        P(("energy", "sect"), None, "slab", None),
        P(("energy", "sect"), None, "slab", None),
        P(("energy", "sect"), None, "slab", None),
    )
    out_specs = P(("energy", "sect"), "slab", None)
    return jax.shard_map(
        per_device, mesh=mesh, in_specs=in_specs, out_specs=out_specs, check_vma=False
    )
```

```python
import functools

import jax
import jax.numpy as jnp
from jax import lax
from jax.experimental import pallas as pl
from jax.experimental.pallas import tpu as pltpu
from jax.sharding import PartitionSpec as P


def from_behind(block, axis, distance):
    devices = range(lax.axis_size(axis))
    route = [(i - distance, i) for i in devices if i - distance in devices]
    return lax.ppermute(block, axis, route)


MEASURED = {8: (5, 1, 0, 2, 7, 3, 4, 6)}


def group_order(devices):
    middle = devices // 2 + 1 if devices > 2 else 0
    return list(MEASURED.get(devices, [(middle - i) % devices for i in range(devices)]))


def exchange(copies):
    order = group_order(copies.shape[0])
    return lax.all_to_all(copies, "slab", split_axis=0, concat_axis=0, axis_index_groups=[order])


def gather_rows(rows):
    devices = lax.axis_size("slab")
    blocks = exchange(jnp.broadcast_to(rows[None], (devices,) + rows.shape))
    order = group_order(devices)
    return [blocks[order.index(i)] for i in range(devices)]


def complex_apply(matrix, blocks):
    vector = jnp.concatenate(blocks, axis=0)
    rows, half_cols = matrix.shape[0] // 2, vector.shape[1] // 2
    both = jnp.dot(matrix, vector, preferred_element_type=jnp.float32)
    real_part, imag_part = both[:rows], both[rows:]
    return jnp.concatenate(
        [
            real_part[:, :half_cols] - imag_part[:, half_cols:],
            real_part[:, half_cols:] + imag_part[:, :half_cols],
        ],
        axis=1,
    )


def in_order(blocks_ref):
    devices = blocks_ref.shape[0]
    order = group_order(devices)
    return [blocks_ref[order.index(i)] for i in range(devices)]


def hand_out(copies_ref, rows):
    for i in range(copies_ref.shape[0]):
        copies_ref[i] = rows


def bundled(ref, height, src_shape):
    return ref.at[pl.ds(0, height)], ref.at[pl.ds(height, height)], ref.at[pl.ds(2 * height, src_shape[0]), pl.ds(0, src_shape[1])]


def prepare_kernel(src_ref, forward_ref, inverse_ref, upper_ref, bundle_ref, upper_out_ref, copies_ref, sems):
    forward_part, inverse_part, src_part = bundled(bundle_ref, forward_ref.shape[0], src_ref.shape)
    both = [(src_ref, src_part), (inverse_ref, inverse_part)]
    first_only = [(upper_ref, upper_out_ref)] + [(src_ref, copies_ref.at[i]) for i in range(copies_ref.shape[0])]
    second_only = [(forward_ref, forward_part)]

    def bring(pairs):
        moves = [pltpu.make_async_copy(a, b, sems.at[i]) for i, (a, b) in enumerate(pairs)]
        for move in moves:
            move.start()
        for move in moves:
            move.wait()

    first = lax.axis_index("sect") == 0

    @pl.when(first)
    def _():
        bring(first_only + both)

    @pl.when(jnp.logical_not(first))
    def _():
        bring(second_only + both)


def forward_kernel(height, other_ref, blocks_ref, copies_ref):
    other_forward, _, other_src = bundled(other_ref, height, blocks_ref.shape[1:])
    first = lax.axis_index("sect") == 0

    @pl.when(first)
    def _():
        made = other_src[...].astype(jnp.float32) + complex_apply(other_forward[...], in_order(blocks_ref))
        hand_out(copies_ref, made.astype(copies_ref.dtype))

    @pl.when(jnp.logical_not(first))
    def _():
        hand_out(copies_ref, other_src[...])


def wave_kernel(height, other_ref, bundle_ref, blocks_ref, copies_ref):
    _, other_inverse, _ = bundled(other_ref, height, blocks_ref.shape[1:])
    own_forward, _, own_src = bundled(bundle_ref, height, blocks_ref.shape[1:])
    first = lax.axis_index("sect") == 0

    @pl.when(first)
    def _():
        made = complex_apply(other_inverse[...], in_order(blocks_ref))
        hand_out(copies_ref, -made.astype(copies_ref.dtype))

    @pl.when(jnp.logical_not(first))
    def _():
        made = own_src[...].astype(jnp.float32) + complex_apply(own_forward[...], in_order(blocks_ref))
        hand_out(copies_ref, made.astype(copies_ref.dtype))


def last_kernel(height, bundle_ref, upper_ref, src_blocks_ref, blocks_ref, out_ref):
    _, inverse, _ = bundled(bundle_ref, height, blocks_ref.shape[1:])
    first = lax.axis_index("sect") == 0

    @pl.when(first)
    def _():
        made = complex_apply(inverse[...], in_order(src_blocks_ref)) + complex_apply(upper_ref[...], in_order(blocks_ref))
        out_ref[...] = made.astype(out_ref.dtype)

    @pl.when(jnp.logical_not(first))
    def _():
        out_ref[...] = complex_apply(inverse[...], in_order(blocks_ref)).astype(out_ref.dtype)


def two_sections(src, forward, inverse, upper):
    devices = lax.axis_size("slab")
    height, order = forward.shape
    vmem = pl.BlockSpec(memory_space=pltpu.VMEM)
    small = pltpu.CompilerParams(vmem_limit_bytes=8 * 1024 * 1024)
    copies_shape = jax.ShapeDtypeStruct((devices,) + src.shape, src.dtype)
    bundle_shape = jax.ShapeDtypeStruct((2 * height + src.shape[0], order), src.dtype)
    bundle, upper, copies = pl.pallas_call(
        prepare_kernel,
        in_specs=[pl.BlockSpec(memory_space=pltpu.HBM)] * 4,
        out_specs=[vmem] * 3,
        out_shape=[bundle_shape, jax.ShapeDtypeStruct(upper.shape, upper.dtype), copies_shape],
        scratch_shapes=[pltpu.SemaphoreType.DMA((devices + 3,))],
        compiler_params=small,
        name="prepare",
    )(*(pltpu.with_memory_space_constraint(array, pltpu.HBM) for array in (src, forward, inverse, upper)))
    other = lax.ppermute(bundle, "sect", [(0, 1), (1, 0)])
    src_blocks = exchange(copies)
    other, src_blocks = lax.optimization_barrier((other, src_blocks))

    def local(kernel, out_shape, *operands):
        return pl.pallas_call(
            functools.partial(kernel, height),
            in_specs=[vmem] * len(operands),
            out_specs=vmem,
            out_shape=out_shape,
            compiler_params=small,
        )(*operands)

    second = exchange(local(forward_kernel, copies_shape, other, src_blocks))
    third = exchange(local(wave_kernel, copies_shape, other, bundle, second))
    out_shape = jax.ShapeDtypeStruct(src.shape, src.dtype)
    return local(last_kernel, out_shape, bundle, upper, src_blocks, third)


def many_sections(src, forward, inverse, upper):
    sections = lax.axis_size("sect")
    src_float = src.astype(jnp.float32)

    def forward_segment(segment_no, current):
        inflow = from_behind(current, "sect", 1)
        return (src_float + complex_apply(forward, gather_rows(inflow))).astype(jnp.bfloat16)

    forward_rows = lax.fori_loop(1, sections, forward_segment, src)
    scaled = complex_apply(inverse, gather_rows(forward_rows))

    def backward_segment(segment_no, current):
        outflow = from_behind(current, "sect", -1)
        return (scaled - complex_apply(upper, gather_rows(outflow))).astype(jnp.bfloat16)

    return lax.fori_loop(1, sections, backward_segment, scaled.astype(jnp.bfloat16))


def per_device(source, forward_mult, schur_inverse, upper_mult):
    src = source[0]
    forward, inverse, upper = (m[0].reshape(-1, m.shape[-1]) for m in (forward_mult, schur_inverse, upper_mult))
    run = two_sections if lax.axis_size("sect") == 2 else many_sections
    return run(src, forward, inverse, upper)[None]


def solution(mesh):
    in_specs = (
        P(("energy", "sect"), "slab", None),
        P(("energy", "sect"), None, "slab", None),
        P(("energy", "sect"), None, "slab", None),
        P(("energy", "sect"), None, "slab", None),
    )
    out_specs = P(("energy", "sect"), "slab", None)
    return jax.shard_map(
        per_device, mesh=mesh, in_specs=in_specs, out_specs=out_specs, check_vma=False
    )
```

```python
import functools

import jax
import jax.numpy as jnp
from jax import lax
from jax.experimental import pallas as pl
from jax.experimental.pallas import tpu as pltpu
from jax.sharding import PartitionSpec as P


def from_behind(block, axis, distance):
    devices = range(lax.axis_size(axis))
    route = [(i - distance, i) for i in devices if i - distance in devices]
    return lax.ppermute(block, axis, route)


MEASURED = {8: (5, 1, 0, 2, 7, 3, 4, 6)}


def group_order(devices):
    middle = devices // 2 + 1 if devices > 2 else 0
    return list(MEASURED.get(devices, [(middle - i) % devices for i in range(devices)]))


def exchange(copies):
    order = group_order(copies.shape[0])
    return lax.all_to_all(copies, "slab", split_axis=0, concat_axis=0, axis_index_groups=[order])


def gather_rows(rows):
    devices = lax.axis_size("slab")
    blocks = exchange(jnp.broadcast_to(rows[None], (devices,) + rows.shape))
    order = group_order(devices)
    return [blocks[order.index(i)] for i in range(devices)]


def combined(both):
    rows, half_cols = both.shape[0] // 2, both.shape[1] // 2
    real_part, imag_part = both[:rows], both[rows:]
    return jnp.concatenate(
        [
            real_part[:, :half_cols] - imag_part[:, half_cols:],
            real_part[:, half_cols:] + imag_part[:, :half_cols],
        ],
        axis=1,
    )


def product(matrix, blocks):
    return jnp.dot(matrix, jnp.concatenate(blocks, axis=0), preferred_element_type=jnp.float32)


def complex_apply(matrix, blocks):
    return combined(product(matrix, blocks))


def in_order(blocks_ref):
    devices = blocks_ref.shape[0]
    order = group_order(devices)
    return [blocks_ref[order.index(i)] for i in range(devices)]


def hand_out(copies_ref, rows):
    for i in range(copies_ref.shape[0]):
        copies_ref[i] = rows


def bundled(ref, height, src_shape):
    return ref.at[pl.ds(0, height)], ref.at[pl.ds(height, height)], ref.at[pl.ds(2 * height, src_shape[0]), pl.ds(0, src_shape[1])]


def pieces(from_ref, to_ref):
    rows = from_ref.shape[0] // 2
    return [(from_ref.at[pl.ds(i * rows, rows)], to_ref.at[pl.ds(i * rows, rows)]) for i in range(2)]


def prepare_kernel(src_ref, forward_ref, inverse_ref, upper_ref, bundle_ref, upper_out_ref, copies_ref, sems):
    forward_part, inverse_part, src_part = bundled(bundle_ref, forward_ref.shape[0], src_ref.shape)

    def bring(pairs):
        moves = [pltpu.make_async_copy(a, b, sems.at[i]) for i, (a, b) in enumerate(pairs)]
        for move in moves:
            move.start()
        return moves

    first = lax.axis_index("sect") == 0

    @pl.when(first)
    def _():
        moves = bring([(src_ref, copies_ref.at[0]), (inverse_ref, inverse_part), (upper_ref, upper_out_ref)])
        moves[0].wait()
        rows = copies_ref[0]
        src_part[...] = rows
        for i in range(1, copies_ref.shape[0]):
            copies_ref[i] = rows
        for move in moves[1:]:
            move.wait()

    @pl.when(jnp.logical_not(first))
    def _():
        halves = pieces(forward_ref, forward_part) + pieces(inverse_ref, inverse_part)
        for move in bring(halves + [(src_ref, src_part)]):
            move.wait()


def forward_kernel(height, other_ref, blocks_ref, copies_ref):
    other_forward, _, other_src = bundled(other_ref, height, blocks_ref.shape[1:])
    first = lax.axis_index("sect") == 0

    @pl.when(first)
    def _():
        made = other_src[...].astype(jnp.float32) + complex_apply(other_forward[...], in_order(blocks_ref))
        hand_out(copies_ref, made.astype(copies_ref.dtype))

    @pl.when(jnp.logical_not(first))
    def _():
        hand_out(copies_ref, other_src[...])


def wave_kernel(height, other_ref, bundle_ref, blocks_ref, copies_ref):
    _, other_inverse, _ = bundled(other_ref, height, blocks_ref.shape[1:])
    own_forward, _, own_src = bundled(bundle_ref, height, blocks_ref.shape[1:])
    first = lax.axis_index("sect") == 0

    @pl.when(first)
    def _():
        made = complex_apply(other_inverse[...], in_order(blocks_ref))
        hand_out(copies_ref, -made.astype(copies_ref.dtype))

    @pl.when(jnp.logical_not(first))
    def _():
        made = own_src[...].astype(jnp.float32) + complex_apply(own_forward[...], in_order(blocks_ref))
        hand_out(copies_ref, made.astype(copies_ref.dtype))


def last_kernel(height, bundle_ref, upper_ref, src_blocks_ref, blocks_ref, out_ref):
    _, inverse, _ = bundled(bundle_ref, height, blocks_ref.shape[1:])
    first = lax.axis_index("sect") == 0

    @pl.when(first)
    def _():
        both = product(inverse[...], in_order(src_blocks_ref)) + product(upper_ref[...], in_order(blocks_ref))
        out_ref[...] = combined(both).astype(out_ref.dtype)

    @pl.when(jnp.logical_not(first))
    def _():
        out_ref[...] = complex_apply(inverse[...], in_order(blocks_ref)).astype(out_ref.dtype)


def two_sections(src, forward, inverse, upper):
    devices = lax.axis_size("slab")
    height, order = forward.shape
    vmem = pl.BlockSpec(memory_space=pltpu.VMEM)
    small = pltpu.CompilerParams(vmem_limit_bytes=8 * 1024 * 1024)
    copies_shape = jax.ShapeDtypeStruct((devices,) + src.shape, src.dtype)
    bundle_shape = jax.ShapeDtypeStruct((2 * height + src.shape[0], order), src.dtype)
    bundle, upper, copies = pl.pallas_call(
        prepare_kernel,
        in_specs=[pl.BlockSpec(memory_space=pltpu.HBM)] * 4,
        out_specs=[vmem] * 3,
        out_shape=[bundle_shape, jax.ShapeDtypeStruct(upper.shape, upper.dtype), copies_shape],
        scratch_shapes=[pltpu.SemaphoreType.DMA((5,))],
        compiler_params=small,
        name="prepare",
    )(*(pltpu.with_memory_space_constraint(array, pltpu.HBM) for array in (src, forward, inverse, upper)))
    other = lax.ppermute(bundle, "sect", [(0, 1), (1, 0)])
    src_blocks = exchange(copies)
    other, src_blocks = lax.optimization_barrier((other, src_blocks))

    def local(kernel, out_shape, *operands):
        return pl.pallas_call(
            functools.partial(kernel, height),
            in_specs=[vmem] * len(operands),
            out_specs=vmem,
            out_shape=out_shape,
            compiler_params=small,
        )(*operands)

    second = exchange(local(forward_kernel, copies_shape, other, src_blocks))
    third = exchange(local(wave_kernel, copies_shape, other, bundle, second))
    out_shape = jax.ShapeDtypeStruct(src.shape, src.dtype)
    return local(last_kernel, out_shape, bundle, upper, src_blocks, third)


def many_sections(src, forward, inverse, upper):
    sections = lax.axis_size("sect")
    src_float = src.astype(jnp.float32)

    def forward_segment(segment_no, current):
        inflow = from_behind(current, "sect", 1)
        return (src_float + complex_apply(forward, gather_rows(inflow))).astype(jnp.bfloat16)

    forward_rows = lax.fori_loop(1, sections, forward_segment, src)
    scaled = complex_apply(inverse, gather_rows(forward_rows))

    def backward_segment(segment_no, current):
        outflow = from_behind(current, "sect", -1)
        return (scaled - complex_apply(upper, gather_rows(outflow))).astype(jnp.bfloat16)

    return lax.fori_loop(1, sections, backward_segment, scaled.astype(jnp.bfloat16))


def per_device(source, forward_mult, schur_inverse, upper_mult):
    src = source[0]
    forward, inverse, upper = (m[0].reshape(-1, m.shape[-1]) for m in (forward_mult, schur_inverse, upper_mult))
    run = two_sections if lax.axis_size("sect") == 2 else many_sections
    return run(src, forward, inverse, upper)[None]


def solution(mesh):
    in_specs = (
        P(("energy", "sect"), "slab", None),
        P(("energy", "sect"), None, "slab", None),
        P(("energy", "sect"), None, "slab", None),
        P(("energy", "sect"), None, "slab", None),
    )
    out_specs = P(("energy", "sect"), "slab", None)
    return jax.shard_map(
        per_device, mesh=mesh, in_specs=in_specs, out_specs=out_specs, check_vma=False
    )
```

```python
import functools

import jax
import jax.numpy as jnp
from jax import lax
from jax.experimental import pallas as pl
from jax.experimental.pallas import tpu as pltpu
from jax.sharding import PartitionSpec as P


def from_behind(block, axis, distance):
    devices = range(lax.axis_size(axis))
    route = [(i - distance, i) for i in devices if i - distance in devices]
    return lax.ppermute(block, axis, route)


MEASURED = {8: (5, 1, 0, 2, 7, 3, 4, 6)}


def group_order(devices):
    middle = devices // 2 + 1 if devices > 2 else 0
    return list(MEASURED.get(devices, [(middle - i) % devices for i in range(devices)]))


def exchange(copies):
    order = group_order(copies.shape[0])
    return lax.all_to_all(copies, "slab", split_axis=0, concat_axis=0, axis_index_groups=[order])


def gather_rows(rows):
    devices = lax.axis_size("slab")
    blocks = exchange(jnp.broadcast_to(rows[None], (devices,) + rows.shape))
    order = group_order(devices)
    return [blocks[order.index(i)] for i in range(devices)]


def complex_apply(matrix, blocks):
    return combined(jnp.dot(matrix, jnp.concatenate(blocks, axis=0), preferred_element_type=jnp.float32))


def combined(both):
    rows, half_cols = both.shape[0] // 2, both.shape[1] // 2
    real_part, imag_part = both[:rows], both[rows:]
    return jnp.concatenate(
        [
            real_part[:, :half_cols] - imag_part[:, half_cols:],
            real_part[:, half_cols:] + imag_part[:, :half_cols],
        ],
        axis=1,
    )


def in_order(blocks_ref):
    devices = blocks_ref.shape[0]
    order = group_order(devices)
    return [blocks_ref[order.index(i)] for i in range(devices)]


def hand_out(copies_ref, rows):
    for i in range(copies_ref.shape[0]):
        copies_ref[i] = rows


def bundled(ref, height, src_shape):
    return ref.at[pl.ds(0, height)], ref.at[pl.ds(height, height)], ref.at[pl.ds(2 * height, src_shape[0]), pl.ds(0, src_shape[1])]


def prepare_kernel(src_ref, forward_ref, inverse_ref, upper_ref, bundle_ref, upper_out_ref, copies_ref, sems):
    forward_part, inverse_part, src_part = bundled(bundle_ref, forward_ref.shape[0], src_ref.shape)

    def bring(pairs):
        moves = [pltpu.make_async_copy(a, b, sems.at[i]) for i, (a, b) in enumerate(pairs)]
        for move in moves:
            move.start()
        return moves

    first = lax.axis_index("sect") == 0

    @pl.when(first)
    def _():
        moves = bring([(src_ref, copies_ref.at[0]), (inverse_ref, inverse_part), (upper_ref, upper_out_ref)])
        moves[0].wait()
        rows = copies_ref[0]
        src_part[...] = rows
        for i in range(1, copies_ref.shape[0]):
            copies_ref[i] = rows
        for move in moves[1:]:
            move.wait()

    @pl.when(jnp.logical_not(first))
    def _():
        for move in bring([(forward_ref, forward_part), (inverse_ref, inverse_part), (src_ref, src_part)]):
            move.wait()


def forward_kernel(height, other_ref, bundle_ref, blocks_ref, copies_ref, scaled_ref):
    other_forward, _, other_src = bundled(other_ref, height, blocks_ref.shape[1:])
    _, inverse, _ = bundled(bundle_ref, height, blocks_ref.shape[1:])
    first = lax.axis_index("sect") == 0

    @pl.when(first)
    def _():
        stacked = jnp.concatenate([other_forward[...], inverse[...]], axis=0)
        both = jnp.dot(stacked, jnp.concatenate(in_order(blocks_ref), axis=0), preferred_element_type=jnp.float32)
        made = other_src[...].astype(jnp.float32) + combined(both[:height])
        hand_out(copies_ref, made.astype(copies_ref.dtype))
        scaled_ref[...] = combined(both[height:])

    @pl.when(jnp.logical_not(first))
    def _():
        hand_out(copies_ref, other_src[...])


def wave_kernel(height, other_ref, bundle_ref, blocks_ref, copies_ref):
    _, other_inverse, _ = bundled(other_ref, height, blocks_ref.shape[1:])
    own_forward, _, own_src = bundled(bundle_ref, height, blocks_ref.shape[1:])
    first = lax.axis_index("sect") == 0

    @pl.when(first)
    def _():
        made = complex_apply(other_inverse[...], in_order(blocks_ref))
        hand_out(copies_ref, -made.astype(copies_ref.dtype))

    @pl.when(jnp.logical_not(first))
    def _():
        made = own_src[...].astype(jnp.float32) + complex_apply(own_forward[...], in_order(blocks_ref))
        hand_out(copies_ref, made.astype(copies_ref.dtype))


def last_kernel(height, bundle_ref, upper_ref, scaled_ref, blocks_ref, out_ref):
    _, inverse, _ = bundled(bundle_ref, height, blocks_ref.shape[1:])
    first = lax.axis_index("sect") == 0

    @pl.when(first)
    def _():
        made = scaled_ref[...] + complex_apply(upper_ref[...], in_order(blocks_ref))
        out_ref[...] = made.astype(out_ref.dtype)

    @pl.when(jnp.logical_not(first))
    def _():
        out_ref[...] = complex_apply(inverse[...], in_order(blocks_ref)).astype(out_ref.dtype)


def two_sections(src, forward, inverse, upper):
    devices = lax.axis_size("slab")
    height, order = forward.shape
    vmem = pl.BlockSpec(memory_space=pltpu.VMEM)
    small = pltpu.CompilerParams(vmem_limit_bytes=8 * 1024 * 1024)
    copies_shape = jax.ShapeDtypeStruct((devices,) + src.shape, src.dtype)
    bundle_shape = jax.ShapeDtypeStruct((2 * height + src.shape[0], order), src.dtype)
    bundle, upper, copies = pl.pallas_call(
        prepare_kernel,
        in_specs=[pl.BlockSpec(memory_space=pltpu.HBM)] * 4,
        out_specs=[vmem] * 3,
        out_shape=[bundle_shape, jax.ShapeDtypeStruct(upper.shape, upper.dtype), copies_shape],
        scratch_shapes=[pltpu.SemaphoreType.DMA((3,))],
        compiler_params=small,
        name="prepare",
    )(*(pltpu.with_memory_space_constraint(array, pltpu.HBM) for array in (src, forward, inverse, upper)))
    other = lax.ppermute(bundle, "sect", [(0, 1), (1, 0)])
    src_blocks = exchange(copies)
    other, src_blocks = lax.optimization_barrier((other, src_blocks))

    def local(kernel, out_shape, *operands):
        return pl.pallas_call(
            functools.partial(kernel, height),
            in_specs=[vmem] * len(operands),
            out_specs=jax.tree.map(lambda _: vmem, out_shape),
            out_shape=out_shape,
            compiler_params=small,
        )(*operands)

    scaled_shape = jax.ShapeDtypeStruct(src.shape, jnp.float32)
    copies, scaled = local(forward_kernel, (copies_shape, scaled_shape), other, bundle, src_blocks)
    second = exchange(copies)
    third = exchange(local(wave_kernel, copies_shape, other, bundle, second))
    out_shape = jax.ShapeDtypeStruct(src.shape, src.dtype)
    return local(last_kernel, out_shape, bundle, upper, scaled, third)


def many_sections(src, forward, inverse, upper):
    sections = lax.axis_size("sect")
    src_float = src.astype(jnp.float32)

    def forward_segment(segment_no, current):
        inflow = from_behind(current, "sect", 1)
        return (src_float + complex_apply(forward, gather_rows(inflow))).astype(jnp.bfloat16)

    forward_rows = lax.fori_loop(1, sections, forward_segment, src)
    scaled = complex_apply(inverse, gather_rows(forward_rows))

    def backward_segment(segment_no, current):
        outflow = from_behind(current, "sect", -1)
        return (scaled - complex_apply(upper, gather_rows(outflow))).astype(jnp.bfloat16)

    return lax.fori_loop(1, sections, backward_segment, scaled.astype(jnp.bfloat16))


def per_device(source, forward_mult, schur_inverse, upper_mult):
    src = source[0]
    forward, inverse, upper = (m[0].reshape(-1, m.shape[-1]) for m in (forward_mult, schur_inverse, upper_mult))
    run = two_sections if lax.axis_size("sect") == 2 else many_sections
    return run(src, forward, inverse, upper)[None]


def solution(mesh):
    in_specs = (
        P(("energy", "sect"), "slab", None),
        P(("energy", "sect"), None, "slab", None),
        P(("energy", "sect"), None, "slab", None),
        P(("energy", "sect"), None, "slab", None),
    )
    out_specs = P(("energy", "sect"), "slab", None)
    return jax.shard_map(
        per_device, mesh=mesh, in_specs=in_specs, out_specs=out_specs, check_vma=False
    )
```

```python
import functools

import jax
import jax.numpy as jnp
from jax import lax
from jax.experimental import pallas as pl
from jax.experimental.pallas import tpu as pltpu
from jax.sharding import PartitionSpec as P


def from_behind(block, axis, distance):
    devices = range(lax.axis_size(axis))
    route = [(i - distance, i) for i in devices if i - distance in devices]
    return lax.ppermute(block, axis, route)


MEASURED = {8: (5, 1, 0, 2, 7, 3, 4, 6)}


def group_order(devices):
    middle = devices // 2 + 1 if devices > 2 else 0
    return list(MEASURED.get(devices, [(middle - i) % devices for i in range(devices)]))


def exchange(copies):
    order = group_order(copies.shape[0])
    return lax.all_to_all(copies, "slab", split_axis=0, concat_axis=0, axis_index_groups=[order])


def gather_rows(rows):
    devices = lax.axis_size("slab")
    blocks = exchange(jnp.broadcast_to(rows[None], (devices,) + rows.shape))
    order = group_order(devices)
    return [blocks[order.index(i)] for i in range(devices)]


def complex_apply(matrix, blocks):
    return combined(jnp.dot(matrix, jnp.concatenate(blocks, axis=0), preferred_element_type=jnp.float32))


def combined(both):
    rows, half_cols = both.shape[0] // 2, both.shape[1] // 2
    real_part, imag_part = both[:rows], both[rows:]
    return jnp.concatenate(
        [
            real_part[:, :half_cols] - imag_part[:, half_cols:],
            real_part[:, half_cols:] + imag_part[:, :half_cols],
        ],
        axis=1,
    )


def in_order(blocks_ref):
    devices = blocks_ref.shape[0]
    order = group_order(devices)
    return [blocks_ref[order.index(i)] for i in range(devices)]


def hand_out(copies_ref, rows):
    for i in range(copies_ref.shape[0]):
        copies_ref[i] = rows


def bundled(ref, height, src_shape):
    return ref.at[pl.ds(0, height)], ref.at[pl.ds(height, height)], ref.at[pl.ds(2 * height, src_shape[0]), pl.ds(0, src_shape[1])]


def pieces(from_ref, to_ref):
    rows = from_ref.shape[0] // 2
    return [(from_ref.at[pl.ds(i * rows, rows)], to_ref.at[pl.ds(i * rows, rows)]) for i in range(2)]


def prepare_kernel(src_ref, forward_ref, inverse_ref, upper_ref, bundle_ref, upper_out_ref, copies_ref, sems):
    forward_part, inverse_part, src_part = bundled(bundle_ref, forward_ref.shape[0], src_ref.shape)

    def bring(pairs):
        moves = [pltpu.make_async_copy(a, b, sems.at[i]) for i, (a, b) in enumerate(pairs)]
        for move in moves:
            move.start()
        return moves

    first = lax.axis_index("sect") == 0

    @pl.when(first)
    def _():
        moves = bring([(src_ref, copies_ref.at[0]), (inverse_ref, inverse_part), (upper_ref, upper_out_ref)])
        moves[0].wait()
        rows = copies_ref[0]
        src_part[...] = rows
        for i in range(1, copies_ref.shape[0]):
            copies_ref[i] = rows
        for move in moves[1:]:
            move.wait()

    @pl.when(jnp.logical_not(first))
    def _():
        halves = pieces(forward_ref, forward_part) + pieces(inverse_ref, inverse_part)
        for move in bring(halves + [(src_ref, src_part)]):
            move.wait()


def forward_kernel(height, other_ref, bundle_ref, blocks_ref, copies_ref, scaled_ref):
    other_forward, _, other_src = bundled(other_ref, height, blocks_ref.shape[1:])
    _, inverse, _ = bundled(bundle_ref, height, blocks_ref.shape[1:])
    first = lax.axis_index("sect") == 0

    @pl.when(first)
    def _():
        stacked = jnp.concatenate([other_forward[...], inverse[...]], axis=0)
        both = jnp.dot(stacked, jnp.concatenate(in_order(blocks_ref), axis=0), preferred_element_type=jnp.float32)
        made = other_src[...].astype(jnp.float32) + combined(both[:height])
        hand_out(copies_ref, made.astype(copies_ref.dtype))
        scaled_ref[...] = combined(both[height:])

    @pl.when(jnp.logical_not(first))
    def _():
        hand_out(copies_ref, other_src[...])


def wave_kernel(height, other_ref, bundle_ref, blocks_ref, copies_ref):
    _, other_inverse, _ = bundled(other_ref, height, blocks_ref.shape[1:])
    own_forward, _, own_src = bundled(bundle_ref, height, blocks_ref.shape[1:])
    first = lax.axis_index("sect") == 0

    @pl.when(first)
    def _():
        made = complex_apply(other_inverse[...], in_order(blocks_ref))
        hand_out(copies_ref, -made.astype(copies_ref.dtype))

    @pl.when(jnp.logical_not(first))
    def _():
        made = own_src[...].astype(jnp.float32) + complex_apply(own_forward[...], in_order(blocks_ref))
        hand_out(copies_ref, made.astype(copies_ref.dtype))


def last_kernel(height, bundle_ref, upper_ref, scaled_ref, blocks_ref, out_ref):
    _, inverse, _ = bundled(bundle_ref, height, blocks_ref.shape[1:])
    first = lax.axis_index("sect") == 0

    @pl.when(first)
    def _():
        made = scaled_ref[...] + complex_apply(upper_ref[...], in_order(blocks_ref))
        out_ref[...] = made.astype(out_ref.dtype)

    @pl.when(jnp.logical_not(first))
    def _():
        out_ref[...] = complex_apply(inverse[...], in_order(blocks_ref)).astype(out_ref.dtype)


def two_sections(src, forward, inverse, upper):
    devices = lax.axis_size("slab")
    height, order = forward.shape
    vmem = pl.BlockSpec(memory_space=pltpu.VMEM)
    small = pltpu.CompilerParams(vmem_limit_bytes=8 * 1024 * 1024)
    copies_shape = jax.ShapeDtypeStruct((devices,) + src.shape, src.dtype)
    bundle_shape = jax.ShapeDtypeStruct((2 * height + src.shape[0], order), src.dtype)
    bundle, upper, copies = pl.pallas_call(
        prepare_kernel,
        in_specs=[pl.BlockSpec(memory_space=pltpu.HBM)] * 4,
        out_specs=[vmem] * 3,
        out_shape=[bundle_shape, jax.ShapeDtypeStruct(upper.shape, upper.dtype), copies_shape],
        scratch_shapes=[pltpu.SemaphoreType.DMA((5,))],
        compiler_params=small,
        name="prepare",
    )(*(pltpu.with_memory_space_constraint(array, pltpu.HBM) for array in (src, forward, inverse, upper)))
    other = lax.ppermute(bundle, "sect", [(0, 1), (1, 0)])
    src_blocks = exchange(copies)
    other, src_blocks = lax.optimization_barrier((other, src_blocks))

    def local(kernel, out_shape, *operands):
        return pl.pallas_call(
            functools.partial(kernel, height),
            in_specs=[vmem] * len(operands),
            out_specs=jax.tree.map(lambda _: vmem, out_shape),
            out_shape=out_shape,
            compiler_params=small,
        )(*operands)

    scaled_shape = jax.ShapeDtypeStruct(src.shape, jnp.float32)
    copies, scaled = local(forward_kernel, (copies_shape, scaled_shape), other, bundle, src_blocks)
    second = exchange(copies)
    third = exchange(local(wave_kernel, copies_shape, other, bundle, second))
    out_shape = jax.ShapeDtypeStruct(src.shape, src.dtype)
    return local(last_kernel, out_shape, bundle, upper, scaled, third)


def many_sections(src, forward, inverse, upper):
    sections = lax.axis_size("sect")
    src_float = src.astype(jnp.float32)

    def forward_segment(segment_no, current):
        inflow = from_behind(current, "sect", 1)
        return (src_float + complex_apply(forward, gather_rows(inflow))).astype(jnp.bfloat16)

    forward_rows = lax.fori_loop(1, sections, forward_segment, src)
    scaled = complex_apply(inverse, gather_rows(forward_rows))

    def backward_segment(segment_no, current):
        outflow = from_behind(current, "sect", -1)
        return (scaled - complex_apply(upper, gather_rows(outflow))).astype(jnp.bfloat16)

    return lax.fori_loop(1, sections, backward_segment, scaled.astype(jnp.bfloat16))


def per_device(source, forward_mult, schur_inverse, upper_mult):
    src = source[0]
    forward, inverse, upper = (m[0].reshape(-1, m.shape[-1]) for m in (forward_mult, schur_inverse, upper_mult))
    run = two_sections if lax.axis_size("sect") == 2 else many_sections
    return run(src, forward, inverse, upper)[None]


def solution(mesh):
    in_specs = (
        P(("energy", "sect"), "slab", None),
        P(("energy", "sect"), None, "slab", None),
        P(("energy", "sect"), None, "slab", None),
        P(("energy", "sect"), None, "slab", None),
    )
    out_specs = P(("energy", "sect"), "slab", None)
    return jax.shard_map(
        per_device, mesh=mesh, in_specs=in_specs, out_specs=out_specs, check_vma=False
    )
```

```python
import functools

import jax
import jax.numpy as jnp
from jax import lax
from jax.experimental import pallas as pl
from jax.experimental.pallas import tpu as pltpu
from jax.sharding import PartitionSpec as P


def from_behind(block, axis, distance):
    devices = range(lax.axis_size(axis))
    route = [(i - distance, i) for i in devices if i - distance in devices]
    return lax.ppermute(block, axis, route)


MEASURED = {8: (5, 3, 0, 2, 7, 1, 4, 6)}


def group_order(devices):
    middle = devices // 2 + 1 if devices > 2 else 0
    return list(MEASURED.get(devices, [(middle - i) % devices for i in range(devices)]))


def exchange(copies):
    order = group_order(copies.shape[0])
    return lax.all_to_all(copies, "slab", split_axis=0, concat_axis=0, axis_index_groups=[order])


def gather_rows(rows):
    devices = lax.axis_size("slab")
    blocks = exchange(jnp.broadcast_to(rows[None], (devices,) + rows.shape))
    order = group_order(devices)
    return [blocks[order.index(i)] for i in range(devices)]


def complex_apply(matrix, blocks):
    vector = jnp.concatenate(blocks, axis=0)
    rows, half_cols = matrix.shape[0] // 2, vector.shape[1] // 2
    both = jnp.dot(matrix, vector, preferred_element_type=jnp.float32)
    real_part, imag_part = both[:rows], both[rows:]
    return jnp.concatenate(
        [
            real_part[:, :half_cols] - imag_part[:, half_cols:],
            real_part[:, half_cols:] + imag_part[:, :half_cols],
        ],
        axis=1,
    )


def in_order(blocks_ref):
    devices = blocks_ref.shape[0]
    order = group_order(devices)
    return [blocks_ref[order.index(i)] for i in range(devices)]


def hand_out(copies_ref, rows):
    for i in range(copies_ref.shape[0]):
        copies_ref[i] = rows


def bundled(ref, height, src_shape):
    return ref.at[pl.ds(0, height)], ref.at[pl.ds(height, height)], ref.at[pl.ds(2 * height, src_shape[0]), pl.ds(0, src_shape[1])]


def prepare_kernel(src_ref, forward_ref, inverse_ref, upper_ref, bundle_ref, upper_out_ref, copies_ref, sems):
    forward_part, inverse_part, src_part = bundled(bundle_ref, forward_ref.shape[0], src_ref.shape)

    def bring(pairs):
        moves = [pltpu.make_async_copy(a, b, sems.at[i]) for i, (a, b) in enumerate(pairs)]
        for move in moves:
            move.start()
        return moves

    first = lax.axis_index("sect") == 0

    @pl.when(first)
    def _():
        moves = bring([(src_ref, copies_ref.at[0]), (inverse_ref, inverse_part), (upper_ref, upper_out_ref)])
        moves[0].wait()
        rows = copies_ref[0]
        src_part[...] = rows
        for i in range(1, copies_ref.shape[0]):
            copies_ref[i] = rows
        for move in moves[1:]:
            move.wait()

    @pl.when(jnp.logical_not(first))
    def _():
        for move in bring([(forward_ref, forward_part), (inverse_ref, inverse_part), (src_ref, src_part)]):
            move.wait()


def forward_kernel(height, other_ref, blocks_ref, copies_ref):
    other_forward, _, other_src = bundled(other_ref, height, blocks_ref.shape[1:])
    first = lax.axis_index("sect") == 0

    @pl.when(first)
    def _():
        made = other_src[...].astype(jnp.float32) + complex_apply(other_forward[...], in_order(blocks_ref))
        hand_out(copies_ref, made.astype(copies_ref.dtype))

    @pl.when(jnp.logical_not(first))
    def _():
        hand_out(copies_ref, other_src[...])


def wave_kernel(height, other_ref, bundle_ref, blocks_ref, copies_ref):
    _, other_inverse, _ = bundled(other_ref, height, blocks_ref.shape[1:])
    own_forward, _, own_src = bundled(bundle_ref, height, blocks_ref.shape[1:])
    first = lax.axis_index("sect") == 0

    @pl.when(first)
    def _():
        made = complex_apply(other_inverse[...], in_order(blocks_ref))
        hand_out(copies_ref, -made.astype(copies_ref.dtype))

    @pl.when(jnp.logical_not(first))
    def _():
        made = own_src[...].astype(jnp.float32) + complex_apply(own_forward[...], in_order(blocks_ref))
        hand_out(copies_ref, made.astype(copies_ref.dtype))


def last_kernel(height, bundle_ref, upper_ref, src_blocks_ref, blocks_ref, out_ref):
    _, inverse, _ = bundled(bundle_ref, height, blocks_ref.shape[1:])
    first = lax.axis_index("sect") == 0

    @pl.when(first)
    def _():
        made = complex_apply(inverse[...], in_order(src_blocks_ref)) + complex_apply(upper_ref[...], in_order(blocks_ref))
        out_ref[...] = made.astype(out_ref.dtype)

    @pl.when(jnp.logical_not(first))
    def _():
        out_ref[...] = complex_apply(inverse[...], in_order(blocks_ref)).astype(out_ref.dtype)


def two_sections(src, forward, inverse, upper):
    devices = lax.axis_size("slab")
    height, order = forward.shape
    vmem = pl.BlockSpec(memory_space=pltpu.VMEM)
    small = pltpu.CompilerParams(vmem_limit_bytes=8 * 1024 * 1024)
    copies_shape = jax.ShapeDtypeStruct((devices,) + src.shape, src.dtype)
    bundle_shape = jax.ShapeDtypeStruct((2 * height + src.shape[0], order), src.dtype)
    bundle, upper, copies = pl.pallas_call(
        prepare_kernel,
        in_specs=[pl.BlockSpec(memory_space=pltpu.HBM)] * 4,
        out_specs=[vmem] * 3,
        out_shape=[bundle_shape, jax.ShapeDtypeStruct(upper.shape, upper.dtype), copies_shape],
        scratch_shapes=[pltpu.SemaphoreType.DMA((3,))],
        compiler_params=small,
        name="prepare",
    )(*(pltpu.with_memory_space_constraint(array, pltpu.HBM) for array in (src, forward, inverse, upper)))
    other = lax.ppermute(bundle, "sect", [(0, 1), (1, 0)])
    src_blocks = exchange(copies)
    other, src_blocks = lax.optimization_barrier((other, src_blocks))

    def local(kernel, out_shape, *operands):
        return pl.pallas_call(
            functools.partial(kernel, height),
            in_specs=[vmem] * len(operands),
            out_specs=vmem,
            out_shape=out_shape,
            compiler_params=small,
        )(*operands)

    second = exchange(local(forward_kernel, copies_shape, other, src_blocks))
    third = exchange(local(wave_kernel, copies_shape, other, bundle, second))
    out_shape = jax.ShapeDtypeStruct(src.shape, src.dtype)
    return local(last_kernel, out_shape, bundle, upper, src_blocks, third)


def many_sections(src, forward, inverse, upper):
    sections = lax.axis_size("sect")
    src_float = src.astype(jnp.float32)

    def forward_segment(segment_no, current):
        inflow = from_behind(current, "sect", 1)
        return (src_float + complex_apply(forward, gather_rows(inflow))).astype(jnp.bfloat16)

    forward_rows = lax.fori_loop(1, sections, forward_segment, src)
    scaled = complex_apply(inverse, gather_rows(forward_rows))

    def backward_segment(segment_no, current):
        outflow = from_behind(current, "sect", -1)
        return (scaled - complex_apply(upper, gather_rows(outflow))).astype(jnp.bfloat16)

    return lax.fori_loop(1, sections, backward_segment, scaled.astype(jnp.bfloat16))


def per_device(source, forward_mult, schur_inverse, upper_mult):
    src = source[0]
    forward, inverse, upper = (m[0].reshape(-1, m.shape[-1]) for m in (forward_mult, schur_inverse, upper_mult))
    run = two_sections if lax.axis_size("sect") == 2 else many_sections
    return run(src, forward, inverse, upper)[None]


def solution(mesh):
    in_specs = (
        P(("energy", "sect"), "slab", None),
        P(("energy", "sect"), None, "slab", None),
        P(("energy", "sect"), None, "slab", None),
        P(("energy", "sect"), None, "slab", None),
    )
    out_specs = P(("energy", "sect"), "slab", None)
    return jax.shard_map(
        per_device, mesh=mesh, in_specs=in_specs, out_specs=out_specs, check_vma=False
    )
```
